32 devices in a mesh: row: 8 (over y, x, core), col: 4 (over z).
Axes of the slice: x: 2, y: 2, z: 4, core: 2. Of those that a mesh axis runs over, the one named last changes fastest.
Arguments:
- tokens: bfloat16 [1024, 12288], P('row', 'col'), may hold values from -10 to 10
- qkv_weight: bfloat16 [12288, 3, 8192], P('col', None, 'row'), as said below
- out_weight: bfloat16 [8192, 12288], P('row', 'col'), may hold values from -0.0625 to 0.0625
Outputs:
- mixed: bfloat16 [1024, 12288], P('row', 'col')
The draws below stay inside these ranges and needn't reach their ends.
Inputs may be any that keep to these rules, and one draw needn't show every extreme that they name: `qkv_weight`: entries of magnitude at most 3 / sqrt(12288).
All inputs are finite; a program needn't handle non-finite values.
Results may differ from the reference program's by a relative error of at most 0.0055.
Values may be sent and summed in bfloat16 or wider, within the bound.
A program may use at most 128 MiB of HBM per device.

```python
import math
import jax
import jax.numpy as jnp
from jax import lax

D = 12288
HD = 128
HEADS = 64
SEQ = 1024
HW = 8192


def draw_tokens(key, part):
    base_key = jax.random.fold_in(key, 0)
    values = jnp.clip(jax.random.normal(base_key, (SEQ, D), jnp.float32), -6.0, 6.0)
    return values.astype(jnp.bfloat16)


def draw_qkv_weight(key, part):
    query_key, key_key, value_key = jax.random.split(key, 3)
    factor = 1.0 / jnp.sqrt(jnp.float32(D))
    shape = (D, HEADS * HD)
    query_part = jnp.clip(jax.random.normal(query_key, shape, jnp.float32), -3.0, 3.0)
    key_part = jnp.clip(jax.random.normal(key_key, shape, jnp.float32), -3.0, 3.0)
    value_part = jnp.clip(jax.random.normal(value_key, shape, jnp.float32), -3.0, 3.0)
    stacked = jnp.stack([query_part, key_part, value_part], axis=1) * factor
    return stacked.astype(jnp.bfloat16)


def steps_of(key, extent, pieces, least, top_value):
    factor_of, own = 1.0, jax.random.fold_in(key, 6)
    for position, blocks in pieces:
        draws = jnp.exp(jax.random.uniform(jax.random.fold_in(own, position), (blocks,), jnp.float32, least / len(pieces), top_value / len(pieces)))
        factor_of = factor_of * jnp.repeat(draws, extent[position] // blocks).reshape([-1 if axis == position else 1 for axis in range(len(extent))])
    return factor_of


def gaussian(rng, shape, spread, bound, cuts=(), kind=jnp.bfloat16):
    drawn = spread * jax.random.normal(rng, shape, jnp.float32)
    if cuts:
        drawn = drawn * steps_of(rng, shape, cuts, -0.22, 0.18)
    return jnp.clip(drawn, -bound, bound).astype(kind)


def setup_inputs(seed: int = 0) -> dict:
    seeds = jax.random.split(jax.random.key(seed), 4)
    return {
        "tokens": draw_tokens(jax.random.fold_in(seeds[3], 71), 0),
        "qkv_weight": draw_qkv_weight(jax.random.fold_in(seeds[3], 71), 0),
        "out_weight": gaussian(seeds[2], (HW, D), HW ** -0.5, 0.0625, ((0, 8), (1, 4))),
    }


def one_head(stacked):
    query_head, key_head, value_head = stacked
    scores = jnp.dot(query_head, key_head.T, preferred_element_type=jnp.float32) * (1.0 / math.sqrt(HD))
    positions = jnp.arange(SEQ, dtype=jnp.int32)
    causal = positions[:, None] >= positions[None, :]
    scores = jnp.where(causal, scores, -1e+30)
    top = lax.optimization_barrier(jnp.max(scores, axis=1, keepdims=True))
    weights = jnp.where(causal, jnp.exp(scores - top), 0.0)
    total = lax.optimization_barrier(jnp.sum(weights, axis=1, keepdims=True))
    context = jnp.dot(weights.astype(jnp.bfloat16), value_head, preferred_element_type=jnp.float32) / total
    return context

def reference(tokens, qkv_weight, out_weight):
    width = HEADS * HD
    weight_flat = qkv_weight.reshape(D, 3 * width)
    qkv = jnp.dot(tokens, weight_flat, preferred_element_type=jnp.float32).astype(jnp.bfloat16)
    qkv = qkv.reshape(SEQ, 3, HEADS, HD)
    queries = jnp.transpose(qkv[:, 0], (1, 0, 2))
    key_rows = jnp.transpose(qkv[:, 1], (1, 0, 2))
    value_rows = jnp.transpose(qkv[:, 2], (1, 0, 2))
    context = lax.map(one_head, (queries, key_rows, value_rows))
    context = jnp.transpose(context, (1, 0, 2)).reshape(SEQ, width).astype(jnp.bfloat16)
    branch = jnp.dot(context, out_weight, preferred_element_type=jnp.float32)
    return (tokens.astype(jnp.float32) + branch).astype(jnp.bfloat16)
```

```python
from functools import partial
import math

import jax
import jax.numpy as jnp
from jax import lax
from jax.experimental import pallas as pl
from jax.experimental.pallas import tpu as pltpu
from jax.sharding import PartitionSpec as P

HD = 128


def attend_block(q, k, v, first):
    scores = lax.dot_general(q, k, (((1,), (1,)), ((), ())), preferred_element_type=jnp.float32)
    scores = scores * (1.0 / math.sqrt(HD))
    row = lax.broadcasted_iota(jnp.int32, scores.shape, 0) + first
    col = lax.broadcasted_iota(jnp.int32, scores.shape, 1)
    causal = row >= col
    scores = jnp.where(causal, scores, -1e30)
    top = jnp.max(scores, axis=1, keepdims=True)
    weights = jnp.where(causal, jnp.exp(scores - top), 0.0)
    total = jnp.sum(weights, axis=1, keepdims=True)
    update = jnp.dot(weights.astype(jnp.bfloat16), v, preferred_element_type=jnp.float32)
    return (update / total).astype(jnp.bfloat16)


MESH = pl.DeviceIdType.MESH
SKEW = 2
GROUPS = 2


def fused_kernel(n, ranks, tok_ref, w_ref, ow_ref, out_ref, panel, wv, ow, acc, send, recv, final, ctx, swap, arrived, resid,
                 w_sem, own_sem, ts, fs, tr, rs_s, rs_r, cx_s, cx_r, sw_s, sw_r, rw_s, rw_r):
    groups = GROUPS
    tb, depth = tok_ref.shape
    half = w_ref.shape[2] // 2
    wg = half // groups
    chips = ranks // 2
    number = tb * ranks
    pieces = ranks * groups
    blocks = cx_s.shape[2]
    qb = number // blocks
    r = lax.axis_index("row")
    z = lax.axis_index("col")
    core = lax.rem(r, 2)
    chip = r // 2
    cx = lax.rem(chip, 2)
    cy = chip // 2
    partner = chip * 2 + 1 - core

    def peer(p, c):
        px = lax.rem(cx + lax.rem(p, 2), 2)
        py = lax.rem(cy + p // 2, chips // 2)
        return (py * 2 + px) * 2 + lax.rem(core + c, 2)

    def w_copy(d, g, s):
        first = d * half + g * wg
        return pltpu.make_async_copy(w_ref.at[s, :, pl.ds(first, wg)], wv.at[d, g, s], w_sem.at[d, g, s])

    own = pltpu.make_async_copy(tok_ref, panel.at[r], own_sem.at[0])
    own.start()
    for g in range(groups):
        for d in range(2):
            for s in range(3):
                w_copy(d, g, s).start()
    ow_copy = pltpu.make_async_copy(ow_ref, ow, own_sem.at[1])
    ow_copy.start()
    resid_copy = pltpu.make_async_copy(tok_ref, resid, own_sem.at[2])
    resid_copy.start()

    barrier = pltpu.get_barrier_semaphore()
    pl.semaphore_signal(barrier, inc=1, device_id={"row": partner}, device_id_type=MESH)
    for p in range(1, chips):
        pl.semaphore_signal(barrier, inc=1, device_id={"row": peer(p, 0)}, device_id_type=MESH)

    @pl.when(z > 0)
    def _():
        pl.semaphore_signal(barrier, inc=1, device_id={"col": z - 1}, device_id_type=MESH)

    @pl.when(z < n - 1)
    def _():
        pl.semaphore_signal(barrier, inc=1, device_id={"col": z + 1}, device_id_type=MESH)

    pl.semaphore_wait(barrier, chips + jnp.where(z > 0, 1, 0) + jnp.where(z < n - 1, 1, 0))

    def tok_send(p):
        target = partner if p == 0 else peer(p, 0)
        return pltpu.make_async_remote_copy(
            tok_ref, panel.at[r], ts.at[p], tr.at[r], device_id={"row": target}, device_id_type=MESH)

    def tok_forward(p):
        block = panel.at[peer(p, 0)]
        return pltpu.make_async_remote_copy(
            block, block, fs.at[p], tr.at[peer(p, 0)], device_id={"row": partner}, device_id_type=MESH)

    def tok_wait(source):
        block = panel.at[source]
        pltpu.make_async_remote_copy(
            block, block, fs.at[0], tr.at[source], device_id={"row": partner}, device_id_type=MESH).wait_recv()

    early = min(3, chips)
    for p in range(early):
        tok_send(p).start()

    def decode(k):
        lead = 2 * groups
        each = 2 * (chips - 1)
        j = jnp.maximum(k - lead, 0)
        p = jnp.where(k < lead, 0, 1 + lax.rem(j, each) // 2)
        g = jnp.where(k < lead, k // 2, j // each)
        return p, g, lax.rem(k, 2)

    def rs_copy(d, k):
        target = jnp.maximum(z - 1, 0) if d == 0 else jnp.minimum(z + 1, n - 1)
        return pltpu.make_async_remote_copy(
            send.at[d, k], recv.at[d, k], rs_s.at[d, k], rs_r.at[d, k],
            device_id={"col": target}, device_id_type=MESH)

    def work(d, k):
        p, g, c = decode(k)
        source = peer(p, c)
        is_source = (z == n - 1) if d == 0 else (z == 0)
        is_sink = (z == 0) if d == 0 else (z == n - 1)

        @pl.when(k < 2 * groups)
        def _():
            @pl.when(lax.rem(k, 2) == 0)
            def _():
                for s in range(3):
                    pltpu.make_async_copy(
                        w_ref.at[s, :, pl.ds(0, wg)], wv.at[d, g, s], w_sem.at[d, g, s]).wait()

        for s in range(3):
            acc[d, s] = jnp.dot(panel[source], wv[d, g, s], preferred_element_type=jnp.float32)

        @pl.when(jnp.logical_not(is_source))
        def _():
            rs_copy(d, k).wait_recv()

        @pl.when(is_source)
        def _():
            for s in range(3):
                send[d, k, s] = acc[d, s].astype(jnp.bfloat16)

        @pl.when(jnp.logical_not(jnp.logical_or(is_source, is_sink)))
        def _():
            for s in range(3):
                send[d, k, s] = (acc[d, s] + recv[d, k, s].astype(jnp.float32)).astype(jnp.bfloat16)

        @pl.when(is_sink)
        def _():
            rows = pl.ds(pl.multiple_of(source * tb, tb), tb)
            for s in range(3):
                final[g, s, rows, :] = (acc[d, s] + recv[d, k, s].astype(jnp.float32)).astype(jnp.bfloat16)

        @pl.when(jnp.logical_not(is_sink))
        def _():
            rs_copy(d, k).start()

    def step(i, carry):
        @pl.when(i < pieces)
        def _():
            p, g, c = decode(i)

            @pl.when(g == 0)
            def _():
                @pl.when(i == 0)
                def _():
                    own.wait()

                @pl.when(i > 0)
                def _():
                    tok_wait(peer(p, c))

                @pl.when(jnp.logical_and(p > 0, c == 0))
                def _():
                    tok_forward(p).start()

        if chips > early:
            @pl.when(i == 2)
            def _():
                for p in range(early, chips):
                    tok_send(p).start()

        for d in range(2):
            k = i - SKEW * ((n - 1 - z) if d == 0 else z)

            @pl.when(jnp.logical_and(k >= 0, k < pieces))
            def _():
                work(d, k)

        return carry

    lax.fori_loop(0, pieces + SKEW * (n - 1), step, 0)

    def ctx_copy(e, g, b):
        target = jnp.minimum(z + 1, n - 1) if e == 0 else jnp.maximum(z - 1, 0)
        part = ctx.at[e, g, pl.ds(b * qb, qb), :]
        return pltpu.make_async_remote_copy(
            part, part, cx_s.at[e, g, b], cx_r.at[e, g, b], device_id={"col": target}, device_id_type=MESH)

    for e in range(2):
        @pl.when(z == (0 if e == 0 else n - 1))
        def _():
            def group(g, carry):
                for b in range(blocks):
                    first, last = b * qb, (b + 1) * qb
                    for h in range(0, wg, HD):
                        ctx[e, g, first:last, h : h + HD] = attend_block(
                            final[g, 0, first:last, h : h + HD], final[g, 1, :last, h : h + HD],
                            final[g, 2, :last, h : h + HD], first)
                    ctx_copy(e, g, b).start()
                return carry

            lax.fori_loop(0, groups, group, 0)

    def relay(i, carry):
        g, b = i // blocks, lax.rem(i, blocks)
        for e in range(2):
            @pl.when(z != (0 if e == 0 else n - 1))
            def _():
                ctx_copy(e, g, b).wait_recv()

                @pl.when(z != (n - 1 if e == 0 else 0))
                def _():
                    ctx_copy(e, g, b).start()

        return carry

    lax.fori_loop(0, groups * blocks, relay, 0)
    for p in range(1, chips):
        tok_forward(p).wait_send()
    ow_copy.wait()
    wide = ow.shape[1] // 4

    def swap_copy(p):
        return pltpu.make_async_remote_copy(
            panel.at[peer(p, 1)], swap.at[p], sw_s.at[p], sw_r.at[p],
            device_id={"row": partner}, device_id_type=MESH)

    def row_copy(p):
        return pltpu.make_async_remote_copy(
            panel.at[peer(p, 0)], arrived.at[chip], rw_s.at[p], rw_r.at[chip],
            device_id={"row": peer(p, 0)}, device_id_type=MESH)

    def row_wait(p):
        source = peer(p, 0)
        pltpu.make_async_remote_copy(
            arrived.at[source // 2], arrived.at[source // 2], rw_s.at[p], rw_r.at[source // 2],
            device_id={"row": source}, device_id_type=MESH).wait_recv()

    def out_step(t, carry):
        @pl.when(t < chips)
        def _():
            p = chips - 1 - t
            pair = peer(p, 0) // 2
            rows = pl.ds(pl.multiple_of(pair * 2 * tb, 2 * tb), 2 * tb)

            def tile(i, carry):
                cols = pl.ds(pl.multiple_of(i * wide, 128), wide)
                total = jnp.zeros((2 * tb, wide), jnp.float32)
                for e in range(2):
                    for g in range(groups):
                        first = e * half + g * wg
                        total += jnp.dot(ctx[e, g, rows, :], ow[first : first + wg, cols], preferred_element_type=jnp.float32)
                panel[pair * 2, :, cols] = total[:tb].astype(jnp.bfloat16)
                panel[pair * 2 + 1, :, cols] = total[tb:].astype(jnp.bfloat16)
                return carry

            lax.fori_loop(0, 4, tile, 0)
            swap_copy(p).start()

        @pl.when(t >= 1)
        def _():
            p = chips - t
            swap_copy(p).wait_recv()
            mine = peer(p, 0)

            def tile(i, carry):
                cols = pl.ds(pl.multiple_of(i * wide, 128), wide)
                panel[mine, :, cols] = (
                    panel[mine, :, cols].astype(jnp.float32) + swap[p, :, cols].astype(jnp.float32)
                ).astype(jnp.bfloat16)
                return carry

            lax.fori_loop(0, 4, tile, 0)

            @pl.when(p > 0)
            def _():
                row_copy(p).start()

        return carry

    lax.fori_loop(0, chips + 1, out_step, 0)
    resid_copy.wait()
    for p in range(1, chips):
        row_wait(p)

    def finish(i, carry):
        cols = pl.ds(pl.multiple_of(i * wide, 128), wide)
        total = panel[r, :, cols].astype(jnp.float32)
        for p in range(1, chips):
            total += arrived[peer(p, 0) // 2, :, cols].astype(jnp.float32)
        out_ref[:, cols] = (resid[:, cols].astype(jnp.float32) + total).astype(jnp.bfloat16)
        return carry

    lax.fori_loop(0, 4, finish, 0)

    for p in range(chips):
        tok_send(p).wait_send()
        swap_copy(p).wait_send()
    for p in range(1, chips):
        row_copy(p).wait_send()

    def drain(k, carry):
        for d in range(2):
            @pl.when(z != (0 if d == 0 else n - 1))
            def _():
                rs_copy(d, k).wait_send()
        return carry

    lax.fori_loop(0, pieces, drain, 0)

    def drain_ctx(i, carry):
        g, b = i // blocks, lax.rem(i, blocks)
        for e in range(2):
            @pl.when(z != (n - 1 if e == 0 else 0))
            def _():
                ctx_copy(e, g, b).wait_send()
        return carry

    lax.fori_loop(0, groups * blocks, drain_ctx, 0)


def fused_local(tokens, qkv_weight, out_weight):
    n, ranks = lax.axis_size("col"), lax.axis_size("row")
    tb, depth = tokens.shape
    cols = qkv_weight.shape[2]
    wg = cols // 2 // GROUPS
    number = tb * ranks
    pieces = ranks * GROUPS
    blocks = max(1, number // 256)
    planes = jnp.transpose(qkv_weight, (1, 0, 2))
    bf16, f32, dma = jnp.bfloat16, jnp.float32, pltpu.SemaphoreType.DMA
    return pl.pallas_call(
        partial(fused_kernel, n, ranks),
        in_specs=[pl.BlockSpec(memory_space=pl.ANY)] * 3,
        out_specs=pl.BlockSpec(memory_space=pltpu.VMEM),
        out_shape=jax.ShapeDtypeStruct(tokens.shape, bf16),
        scratch_shapes=[
            pltpu.VMEM((ranks, tb, depth), bf16),
            pltpu.VMEM((2, GROUPS, 3, depth, wg), bf16),
            pltpu.VMEM(out_weight.shape, bf16),
            pltpu.VMEM((2, 3, tb, wg), f32),
            pltpu.VMEM((2, pieces, 3, tb, wg), bf16),
            pltpu.VMEM((2, pieces, 3, tb, wg), bf16),
            pltpu.VMEM((GROUPS, 3, number, wg), bf16),
            pltpu.VMEM((2, GROUPS, number, wg), bf16),
            pltpu.VMEM((ranks // 2, tb, depth), bf16),
            pltpu.VMEM((ranks // 2, tb, depth), bf16),
            pltpu.VMEM((tb, depth), bf16),
            dma((2, GROUPS, 3)), dma((3,)), dma((ranks // 2,)), dma((ranks // 2,)), dma((ranks,)),
            dma((2, pieces)), dma((2, pieces)), dma((2, GROUPS, blocks)), dma((2, GROUPS, blocks)),
            dma((ranks // 2,)), dma((ranks // 2,)), dma((ranks // 2,)), dma((ranks // 2,)),
        ],
        compiler_params=pltpu.CompilerParams(
            collective_id=0, has_side_effects=True, vmem_limit_bytes=67043328),
    )(tokens, planes, out_weight)

def tokens_local(tokens, qkv_weight, out_weight):
    n = lax.axis_size("col")
    panel = lax.all_gather(tokens, "row", axis=0, tiled=True)
    depth, _, head_cols = qkv_weight.shape
    count = panel.shape[0] // n
    first = lax.axis_index("col") * count
    heads = head_cols // HD
    product = jnp.dot(panel, qkv_weight.reshape(depth, 3 * head_cols), preferred_element_type=jnp.float32)
    qkv = lax.psum_scatter(product, "col", scatter_dimension=0, tiled=True).astype(jnp.bfloat16)
    q = qkv[:, :head_cols].reshape(count, heads, HD)
    k = lax.all_gather(qkv[:, head_cols : 2 * head_cols], "col", axis=0, tiled=True).reshape(-1, heads, HD)
    v = lax.all_gather(qkv[:, 2 * head_cols :], "col", axis=0, tiled=True).reshape(-1, heads, HD)
    scores = jnp.einsum("qhd,khd->qhk", q, k, preferred_element_type=jnp.float32) * (1.0 / math.sqrt(HD))
    causal = (first + jnp.arange(count)[:, None] >= jnp.arange(k.shape[0])[None, :])[:, None, :]
    scores = jnp.where(causal, scores, -1e30)
    weights = jnp.where(causal, jnp.exp(scores - jnp.max(scores, axis=2, keepdims=True)), 0.0)
    total = jnp.sum(weights, axis=2)
    update = jnp.einsum("qhk,khd->qhd", weights.astype(jnp.bfloat16), v, preferred_element_type=jnp.float32)
    context = (update / total[:, :, None]).reshape(count, head_cols).astype(jnp.bfloat16)
    gathered = lax.all_gather(context, "col", axis=0, tiled=True)
    product = jnp.dot(gathered, out_weight, preferred_element_type=jnp.float32)
    summed = lax.psum_scatter(product, "row", scatter_dimension=0, tiled=True)
    return (tokens.astype(jnp.float32) + summed).astype(jnp.bfloat16)


def local(tokens, qkv_weight, out_weight):
    ranks, width = lax.axis_size("row"), qkv_weight.shape[2]
    if ranks % 4 == 0 and lax.axis_size("col") > 1 and width % (2 * GROUPS * HD) == 0:
        return fused_local(tokens, qkv_weight, out_weight)
    return tokens_local(tokens, qkv_weight, out_weight)


def solution(mesh):
    in_specs = (P("row", "col"), P("col", None, "row"), P("row", "col"))
    out_specs = P("row", "col")
    return jax.shard_map(local, mesh=mesh, in_specs=in_specs, out_specs=out_specs, check_vma=False)
```

```python
from functools import partial
import math

import jax
import jax.numpy as jnp
from jax import lax
from jax.experimental import pallas as pl
from jax.experimental.pallas import tpu as pltpu
from jax.sharding import PartitionSpec as P

HD = 128


def attend_block(q, k, v, first):
    scores = lax.dot_general(q, k, (((1,), (1,)), ((), ())), preferred_element_type=jnp.float32)
    scores = scores * (1.0 / math.sqrt(HD))
    row = lax.broadcasted_iota(jnp.int32, scores.shape, 0) + first
    col = lax.broadcasted_iota(jnp.int32, scores.shape, 1)
    causal = row >= col
    scores = jnp.where(causal, scores, -1e30)
    top = jnp.max(scores, axis=1, keepdims=True)
    weights = jnp.where(causal, jnp.exp(scores - top), 0.0)
    total = jnp.sum(weights, axis=1, keepdims=True)
    update = jnp.dot(weights.astype(jnp.bfloat16), v, preferred_element_type=jnp.float32)
    return (update / total).astype(jnp.bfloat16)


MESH = pl.DeviceIdType.MESH
SKEW = 2
GROUPS = 2


def fused_kernel(n, ranks, tok_ref, w_ref, ow_ref, out_ref, panel, wv, ow, acc, send, recv, final, ctx, swap, arrived, resid,
                 w_sem, own_sem, ts, fs, tr, rs_s, rs_r, cx_s, cx_r, sw_s, sw_r, rw_s, rw_r):
    groups = GROUPS
    tb, depth = tok_ref.shape
    half = w_ref.shape[2] // 2
    wg = half // groups
    chips = ranks // 2
    number = tb * ranks
    pieces = ranks * groups
    blocks = cx_s.shape[2]
    qb = number // blocks
    r = lax.axis_index("row")
    z = lax.axis_index("col")
    core = lax.rem(r, 2)
    chip = r // 2
    cx = lax.rem(chip, 2)
    cy = chip // 2
    partner = chip * 2 + 1 - core

    def peer(p, c):
        px = lax.rem(cx + lax.rem(p, 2), 2)
        py = lax.rem(cy + p // 2, chips // 2)
        return (py * 2 + px) * 2 + lax.rem(core + c, 2)

    def w_copy(d, g, s):
        first = d * half + g * wg
        return pltpu.make_async_copy(w_ref.at[s, :, pl.ds(first, wg)], wv.at[d, g, s], w_sem.at[d, g, s])

    own = pltpu.make_async_copy(tok_ref, panel.at[r], own_sem.at[0])
    own.start()
    for g in range(groups):
        for d in range(2):
            for s in range(3):
                w_copy(d, g, s).start()
    ow_copy = pltpu.make_async_copy(ow_ref, ow, own_sem.at[1])
    ow_copy.start()
    resid_copy = pltpu.make_async_copy(tok_ref, resid, own_sem.at[2])
    resid_copy.start()

    barrier = pltpu.get_barrier_semaphore()
    pl.semaphore_signal(barrier, inc=1, device_id={"row": partner}, device_id_type=MESH)
    for p in range(1, chips):
        pl.semaphore_signal(barrier, inc=1, device_id={"row": peer(p, 0)}, device_id_type=MESH)

    @pl.when(z > 0)
    def _():
        pl.semaphore_signal(barrier, inc=1, device_id={"col": z - 1}, device_id_type=MESH)

    @pl.when(z < n - 1)
    def _():
        pl.semaphore_signal(barrier, inc=1, device_id={"col": z + 1}, device_id_type=MESH)

    pl.semaphore_wait(barrier, chips + jnp.where(z > 0, 1, 0) + jnp.where(z < n - 1, 1, 0))

    def tok_send(p):
        target = partner if p == 0 else peer(p, 0)
        return pltpu.make_async_remote_copy(
            tok_ref, panel.at[r], ts.at[p], tr.at[r], device_id={"row": target}, device_id_type=MESH)

    def tok_forward(p):
        block = panel.at[peer(p, 0)]
        return pltpu.make_async_remote_copy(
            block, block, fs.at[p], tr.at[peer(p, 0)], device_id={"row": partner}, device_id_type=MESH)

    def tok_wait(source):
        block = panel.at[source]
        pltpu.make_async_remote_copy(
            block, block, fs.at[0], tr.at[source], device_id={"row": partner}, device_id_type=MESH).wait_recv()

    early = min(3, chips)
    for p in range(early):
        tok_send(p).start()

    def decode(k):
        lead = 2 * groups
        each = 2 * (chips - 1)
        j = jnp.maximum(k - lead, 0)
        p = jnp.where(k < lead, 0, 1 + lax.rem(j, each) // 2)
        g = jnp.where(k < lead, k // 2, j // each)
        return p, g, lax.rem(k, 2)

    def rs_copy(d, k):
        target = jnp.maximum(z - 1, 0) if d == 0 else jnp.minimum(z + 1, n - 1)
        return pltpu.make_async_remote_copy(
            send.at[d, k], recv.at[d, k], rs_s.at[d, k], rs_r.at[d, k],
            device_id={"col": target}, device_id_type=MESH)

    def work(d, k):
        p, g, c = decode(k)
        source = peer(p, c)
        is_source = (z == n - 1) if d == 0 else (z == 0)
        is_sink = (z == 0) if d == 0 else (z == n - 1)

        @pl.when(k < 2 * groups)
        def _():
            @pl.when(lax.rem(k, 2) == 0)
            def _():
                for s in range(3):
                    pltpu.make_async_copy(
                        w_ref.at[s, :, pl.ds(0, wg)], wv.at[d, g, s], w_sem.at[d, g, s]).wait()

        for s in range(3):
            acc[d, s] = jnp.dot(panel[source], wv[d, g, s], preferred_element_type=jnp.float32)

        @pl.when(jnp.logical_not(is_source))
        def _():
            rs_copy(d, k).wait_recv()

        @pl.when(is_source)
        def _():
            for s in range(3):
                send[d, k, s] = acc[d, s].astype(jnp.bfloat16)

        @pl.when(jnp.logical_not(jnp.logical_or(is_source, is_sink)))
        def _():
            for s in range(3):
                send[d, k, s] = (acc[d, s] + recv[d, k, s].astype(jnp.float32)).astype(jnp.bfloat16)

        @pl.when(is_sink)
        def _():
            rows = pl.ds(pl.multiple_of(source * tb, tb), tb)
            for s in range(3):
                final[g, s, rows, :] = (acc[d, s] + recv[d, k, s].astype(jnp.float32)).astype(jnp.bfloat16)

        @pl.when(jnp.logical_not(is_sink))
        def _():
            rs_copy(d, k).start()

    def ctx_copy(e, g, b):
        target = jnp.minimum(z + 1, n - 1) if e == 0 else jnp.maximum(z - 1, 0)
        part = ctx.at[e, g, pl.ds(b * qb, qb), :]
        return pltpu.make_async_remote_copy(
            part, part, cx_s.at[e, g, b], cx_r.at[e, g, b], device_id={"col": target}, device_id_type=MESH)

    def attend(e, g, b):
        first, last = b * qb, (b + 1) * qb
        for h in range(0, wg, HD):
            ctx[e, g, first:last, h : h + HD] = attend_block(
                final[g, 0, first:last, h : h + HD], final[g, 1, :last, h : h + HD],
                final[g, 2, :last, h : h + HD], first)
        ctx_copy(e, g, b).start()

    ready = 2 * groups + 2 * (chips - 1) + SKEW * (n - 1)

    def step(i, carry):
        @pl.when(i < pieces)
        def _():
            p, g, c = decode(i)

            @pl.when(g == 0)
            def _():
                @pl.when(i == 0)
                def _():
                    own.wait()

                @pl.when(i > 0)
                def _():
                    tok_wait(peer(p, c))

                @pl.when(jnp.logical_and(p > 0, c == 0))
                def _():
                    tok_forward(p).start()

        if chips > early:
            @pl.when(i == 2)
            def _():
                for p in range(early, chips):
                    tok_send(p).start()

        for d in range(2):
            k = i - SKEW * ((n - 1 - z) if d == 0 else z)

            @pl.when(jnp.logical_and(k >= 0, k < pieces))
            def _():
                work(d, k)

        for e in range(2):
            @pl.when(z == (0 if e == 0 else n - 1))
            def _():
                for b in range(blocks):
                    @pl.when(i == ready + b)
                    def _():
                        attend(e, 0, b)

        return carry

    lax.fori_loop(0, max(pieces + SKEW * (n - 1), ready + blocks), step, 0)

    for e in range(2):
        @pl.when(z == (0 if e == 0 else n - 1))
        def _():
            def group(g, carry):
                for b in range(blocks):
                    attend(e, g, b)
                return carry

            lax.fori_loop(1, groups, group, 0)

    def relay(i, carry):
        g, b = i // blocks, lax.rem(i, blocks)
        for e in range(2):
            @pl.when(z != (0 if e == 0 else n - 1))
            def _():
                ctx_copy(e, g, b).wait_recv()

                @pl.when(z != (n - 1 if e == 0 else 0))
                def _():
                    ctx_copy(e, g, b).start()

        return carry

    lax.fori_loop(0, groups * blocks, relay, 0)
    for p in range(1, chips):
        tok_forward(p).wait_send()
    ow_copy.wait()
    wide = ow.shape[1] // 4

    def swap_copy(p):
        return pltpu.make_async_remote_copy(
            panel.at[peer(p, 1)], swap.at[p], sw_s.at[p], sw_r.at[p],
            device_id={"row": partner}, device_id_type=MESH)

    def row_copy(p):
        return pltpu.make_async_remote_copy(
            panel.at[peer(p, 0)], arrived.at[chip], rw_s.at[p], rw_r.at[chip],
            device_id={"row": peer(p, 0)}, device_id_type=MESH)

    def row_wait(p):
        source = peer(p, 0)
        pltpu.make_async_remote_copy(
            arrived.at[source // 2], arrived.at[source // 2], rw_s.at[p], rw_r.at[source // 2],
            device_id={"row": source}, device_id_type=MESH).wait_recv()

    def out_step(t, carry):
        @pl.when(t < chips)
        def _():
            p = chips - 1 - t
            pair = peer(p, 0) // 2
            rows = pl.ds(pl.multiple_of(pair * 2 * tb, 2 * tb), 2 * tb)

            def tile(i, carry):
                cols = pl.ds(pl.multiple_of(i * wide, 128), wide)
                total = jnp.zeros((2 * tb, wide), jnp.float32)
                for e in range(2):
                    for g in range(groups):
                        first = e * half + g * wg
                        total += jnp.dot(ctx[e, g, rows, :], ow[first : first + wg, cols], preferred_element_type=jnp.float32)
                panel[pair * 2, :, cols] = total[:tb].astype(jnp.bfloat16)
                panel[pair * 2 + 1, :, cols] = total[tb:].astype(jnp.bfloat16)
                return carry

            lax.fori_loop(0, 4, tile, 0)
            swap_copy(p).start()

        @pl.when(t >= 1)
        def _():
            p = chips - t
            swap_copy(p).wait_recv()
            mine = peer(p, 0)

            def tile(i, carry):
                cols = pl.ds(pl.multiple_of(i * wide, 128), wide)
                panel[mine, :, cols] = (
                    panel[mine, :, cols].astype(jnp.float32) + swap[p, :, cols].astype(jnp.float32)
                ).astype(jnp.bfloat16)
                return carry

            lax.fori_loop(0, 4, tile, 0)

            @pl.when(p > 0)
            def _():
                row_copy(p).start()

        return carry

    lax.fori_loop(0, chips + 1, out_step, 0)
    resid_copy.wait()
    for p in range(1, chips):
        row_wait(p)

    def finish(i, carry):
        cols = pl.ds(pl.multiple_of(i * wide, 128), wide)
        total = panel[r, :, cols].astype(jnp.float32)
        for p in range(1, chips):
            total += arrived[peer(p, 0) // 2, :, cols].astype(jnp.float32)
        out_ref[:, cols] = (resid[:, cols].astype(jnp.float32) + total).astype(jnp.bfloat16)
        return carry

    lax.fori_loop(0, 4, finish, 0)

    for p in range(chips):
        tok_send(p).wait_send()
        swap_copy(p).wait_send()
    for p in range(1, chips):
        row_copy(p).wait_send()

    def drain(k, carry):
        for d in range(2):
            @pl.when(z != (0 if d == 0 else n - 1))
            def _():
                rs_copy(d, k).wait_send()
        return carry

    lax.fori_loop(0, pieces, drain, 0)

    def drain_ctx(i, carry):
        g, b = i // blocks, lax.rem(i, blocks)
        for e in range(2):
            @pl.when(z != (n - 1 if e == 0 else 0))
            def _():
                ctx_copy(e, g, b).wait_send()
        return carry

    lax.fori_loop(0, groups * blocks, drain_ctx, 0)


def fused_local(tokens, qkv_weight, out_weight):
    n, ranks = lax.axis_size("col"), lax.axis_size("row")
    tb, depth = tokens.shape
    cols = qkv_weight.shape[2]
    wg = cols // 2 // GROUPS
    number = tb * ranks
    pieces = ranks * GROUPS
    blocks = max(1, number // 256)
    planes = jnp.transpose(qkv_weight, (1, 0, 2))
    bf16, f32, dma = jnp.bfloat16, jnp.float32, pltpu.SemaphoreType.DMA
    return pl.pallas_call(
        partial(fused_kernel, n, ranks),
        in_specs=[pl.BlockSpec(memory_space=pl.ANY)] * 3,
        out_specs=pl.BlockSpec(memory_space=pltpu.VMEM),
        out_shape=jax.ShapeDtypeStruct(tokens.shape, bf16),
        scratch_shapes=[
            pltpu.VMEM((ranks, tb, depth), bf16),
            pltpu.VMEM((2, GROUPS, 3, depth, wg), bf16),
            pltpu.VMEM(out_weight.shape, bf16),
            pltpu.VMEM((2, 3, tb, wg), f32),
            pltpu.VMEM((2, pieces, 3, tb, wg), bf16),
            pltpu.VMEM((2, pieces, 3, tb, wg), bf16),
            pltpu.VMEM((GROUPS, 3, number, wg), bf16),
            pltpu.VMEM((2, GROUPS, number, wg), bf16),
            pltpu.VMEM((ranks // 2, tb, depth), bf16),
            pltpu.VMEM((ranks // 2, tb, depth), bf16),
            pltpu.VMEM((tb, depth), bf16),
            dma((2, GROUPS, 3)), dma((3,)), dma((ranks // 2,)), dma((ranks // 2,)), dma((ranks,)),
            dma((2, pieces)), dma((2, pieces)), dma((2, GROUPS, blocks)), dma((2, GROUPS, blocks)),
            dma((ranks // 2,)), dma((ranks // 2,)), dma((ranks // 2,)), dma((ranks // 2,)),
        ],
        compiler_params=pltpu.CompilerParams(
            collective_id=0, has_side_effects=True, vmem_limit_bytes=67043328),
    )(tokens, planes, out_weight)

def tokens_local(tokens, qkv_weight, out_weight):
    n = lax.axis_size("col")
    panel = lax.all_gather(tokens, "row", axis=0, tiled=True)
    depth, _, head_cols = qkv_weight.shape
    count = panel.shape[0] // n
    first = lax.axis_index("col") * count
    heads = head_cols // HD
    product = jnp.dot(panel, qkv_weight.reshape(depth, 3 * head_cols), preferred_element_type=jnp.float32)
    qkv = lax.psum_scatter(product, "col", scatter_dimension=0, tiled=True).astype(jnp.bfloat16)
    q = qkv[:, :head_cols].reshape(count, heads, HD)
    k = lax.all_gather(qkv[:, head_cols : 2 * head_cols], "col", axis=0, tiled=True).reshape(-1, heads, HD)
    v = lax.all_gather(qkv[:, 2 * head_cols :], "col", axis=0, tiled=True).reshape(-1, heads, HD)
    scores = jnp.einsum("qhd,khd->qhk", q, k, preferred_element_type=jnp.float32) * (1.0 / math.sqrt(HD))
    causal = (first + jnp.arange(count)[:, None] >= jnp.arange(k.shape[0])[None, :])[:, None, :]
    scores = jnp.where(causal, scores, -1e30)
    weights = jnp.where(causal, jnp.exp(scores - jnp.max(scores, axis=2, keepdims=True)), 0.0)
    total = jnp.sum(weights, axis=2)
    update = jnp.einsum("qhk,khd->qhd", weights.astype(jnp.bfloat16), v, preferred_element_type=jnp.float32)
    context = (update / total[:, :, None]).reshape(count, head_cols).astype(jnp.bfloat16)
    gathered = lax.all_gather(context, "col", axis=0, tiled=True)
    product = jnp.dot(gathered, out_weight, preferred_element_type=jnp.float32)
    summed = lax.psum_scatter(product, "row", scatter_dimension=0, tiled=True)
    return (tokens.astype(jnp.float32) + summed).astype(jnp.bfloat16)


def local(tokens, qkv_weight, out_weight):
    ranks, width = lax.axis_size("row"), qkv_weight.shape[2]
    if ranks % 4 == 0 and lax.axis_size("col") > 1 and width % (2 * GROUPS * HD) == 0:
        return fused_local(tokens, qkv_weight, out_weight)
    return tokens_local(tokens, qkv_weight, out_weight)


def solution(mesh):
    in_specs = (P("row", "col"), P("col", None, "row"), P("row", "col"))
    out_specs = P("row", "col")
    return jax.shard_map(local, mesh=mesh, in_specs=in_specs, out_specs=out_specs, check_vma=False)
```
